512 devices in a mesh: row: 16 (over z, core), col: 32 (over x, y).
Axes of the slice: x: 4, y: 8, z: 8, core: 2. Of those that a mesh axis runs over, the one named last changes fastest.
Arguments:
- trail_adjoint: float32 [16384, 16384], P('row', 'col'), may hold values from -0.046875 to 0.046875
- panel: float32 [16384, 128], P('row', 'col')
- panel_adjoint: float32 [16384, 128], P('row', 'col'), may hold values from -6 to 6
- inv_diag: float32 [128, 128], replicated, as said below
- panel_index: int32 [1], replicated, may hold values from 832 to 895
Outputs:
- panel_grad: float32 [16384, 128], P('row', 'col')
- diag_grad: float32 [128, 128], P(None, 'col')
The draws below stay inside these ranges and needn't reach their ends.
Inputs may be any that keep to these rules, and one draw needn't show every extreme that they name: inv_diag is lower triangular with a positive diagonal.
All inputs are finite; a program needn't handle non-finite values.
Results may differ from the reference program's by a relative error of at most 0.000075.
Values sent between devices are 32-bit elements; how exact they have to be, the bound alone decides.
No kernel may reach another device: no remote copies, remote signals or barrier semaphores. Data moves between devices by JAX's collectives and lax.ppermute only.
A program may use at most 64 MiB of HBM per device.

```python
import jax
import jax.numpy as jnp
from jax import lax

B = 128
M = 16384
LOC_ROWS = 1024
N_ROW = 16
N_COL = 32


def draw_panel(key, part):
    base_key = jax.random.fold_in(key, 0)
    row_device = (jnp.arange(M) // LOC_ROWS).astype(jnp.float32)
    dev_count = max(M // LOC_ROWS - 1, 1)
    rise_scale = 1.0 + 2.0 * row_device / dev_count
    base_draw = jnp.clip(jax.random.normal(base_key, (M, B), jnp.float32), -4.0, 4.0)
    return (base_draw * rise_scale[:, None] * M ** (-0.25)).astype(jnp.float32)


def draw_inv_diag(key, part):
    first_key, second_key = jax.random.split(key)
    lower_part = 0.5 * jax.random.normal(first_key, (B, B), jnp.float32) / jnp.sqrt(jnp.float32(B))
    diag_values = jnp.exp(jax.random.uniform(second_key, (B,), jnp.float32, jnp.log(0.5), jnp.log(2.0)))
    return (jnp.tril(lower_part, -1) + jnp.diag(diag_values)).astype(jnp.float32)


def level_of(rng, shape, pieces, smallest, top_value):
    gain = 1.0
    for dim, blocks in pieces:
        steps = jax.random.uniform(jax.random.fold_in(jax.random.fold_in(rng, 6), dim), (blocks,), jnp.float32, smallest / len(pieces), top_value / len(pieces))
        gain = gain * jnp.repeat(jnp.exp(steps), shape[dim] // blocks).reshape((-1,) + (1,) * (len(shape) - 1 - dim))
    return gain


def scatter_about(key, dims, deviation, bound, shards=(), kind=jnp.bfloat16):
    level = level_of(key, dims, shards, -0.22, 0.18) if shards else 1.0
    drawn = jax.random.normal(key, dims, jnp.float32) * deviation * level
    return jnp.minimum(jnp.maximum(drawn, -bound), bound).astype(kind)


def setup_inputs(seed: int = 0) -> dict:
    key_of = jax.random.split(jax.random.key(seed), 6)
    trail_adjoint = scatter_about(key_of[0], (M, M), M ** -0.5, 0.046875, ((0, 16), (1, 32)), jnp.float32)
    panel = draw_panel(jax.random.fold_in(key_of[5], 71), 0)
    panel_adjoint = scatter_about(key_of[2], (M, B), 1.0, 6.0, ((0, 16), (1, 32)), jnp.float32)
    inv_diag = draw_inv_diag(jax.random.fold_in(key_of[5], 71), 0)
    panel_index = jax.random.randint(key_of[4], (1,), 832, 896).astype(jnp.int32)
    return {"trail_adjoint": trail_adjoint, "panel": panel, "panel_adjoint": panel_adjoint, "inv_diag": inv_diag, "panel_index": panel_index}


def reference(trail_adjoint, panel, panel_adjoint, inv_diag, panel_index):
    panel_at = panel_index[0]
    block_count = M // B
    blocks_true = jnp.arange(block_count, dtype=jnp.int32)
    row_store = jnp.mod(blocks_true + panel_at + 1, N_ROW).astype(jnp.int32) * (block_count // N_ROW) + blocks_true // N_ROW
    col_store = jnp.mod(blocks_true + panel_at + 1, N_COL).astype(jnp.int32) * (block_count // N_COL) + blocks_true // N_COL
    source = jnp.zeros((block_count,), jnp.int32).at[col_store].set(row_store.astype(jnp.int32))
    panel_blocks = panel.reshape(block_count, B, B)
    column_panel = panel_blocks[source].reshape(M, B)
    product = jnp.dot(trail_adjoint, column_panel, precision=lax.Precision.HIGHEST, preferred_element_type=jnp.float32)
    factor_adjoint = panel_adjoint - 2.0 * product
    panel_grad = jnp.dot(factor_adjoint, inv_diag, precision=lax.Precision.HIGHEST, preferred_element_type=jnp.float32)
    gram = jnp.dot(factor_adjoint.T, panel, precision=lax.Precision.HIGHEST, preferred_element_type=jnp.float32)
    diag_grad = -jnp.dot(inv_diag.T, gram, precision=lax.Precision.HIGHEST, preferred_element_type=jnp.float32)
    return panel_grad, diag_grad
```

```python
import jax
import jax.numpy as jnp
from jax import lax
from jax.sharding import PartitionSpec as P

HIGH = lax.Precision.HIGHEST


def dot(a, b, contract):
    return lax.dot_general(
        a, b, (contract, ((), ())), precision=HIGH, preferred_element_type=jnp.float32
    )


def exchange(value, axis):
    return lax.all_to_all(value, axis, split_axis=0, concat_axis=0)


def body(trail_adjoint, panel, panel_adjoint, inv_diag, panel_index):
    rows_here, thin_cols = panel.shape
    width = inv_diag.shape[0]
    ways_row = lax.axis_size("row")
    ways_col = lax.axis_size("col")
    ratio = ways_col // ways_row
    cols_here = trail_adjoint.shape[1]
    col_here = lax.axis_index("col")
    thin = panel.T
    everywhere = exchange(jnp.broadcast_to(thin[None], (ways_row, thin_cols, rows_here)), "row")
    parts = everywhere.reshape(ways_row, thin_cols, cols_here // width, ratio, width)
    targets = jnp.arange(ways_col, dtype=jnp.int32).reshape(ratio, ways_row)
    offset = jnp.mod(targets - panel_index[0] - 1, ways_col) // ways_row
    offset = offset[:, :, None, None, None]
    chosen = jnp.zeros((ratio, ways_row, thin_cols, cols_here // width, width), jnp.float32)
    for i in range(ratio):
        chosen = jnp.where(offset == i, parts[None, :, :, :, i], chosen)
    chosen = chosen.reshape(ways_col, thin_cols, cols_here)
    sent = jnp.concatenate(
        [chosen, jnp.broadcast_to(thin[None], (ways_col, thin_cols, rows_here))], axis=2
    )
    got = exchange(sent, "col").reshape(width, cols_here + rows_here)
    column_panel = got[:, :cols_here]
    panel_rows = got[:, cols_here:]
    scaled = dot(inv_diag, column_panel, ((0,), (0,)))
    product = dot(scaled, trail_adjoint, ((1,), (1,)))
    my_inverse = lax.dynamic_slice_in_dim(inv_diag, col_here * thin_cols, thin_cols, 0)
    local = dot(my_inverse, panel_adjoint.T, ((0,), (0,))) - 2.0 * product
    diag = -dot(panel_rows, local, ((1,), (1,)))
    both = jnp.concatenate([local, diag], axis=1).reshape(ways_col, thin_cols, rows_here + width)
    total = jnp.sum(exchange(both, "col"), axis=0)
    panel_grad = total[:, :rows_here].T
    mine = jnp.broadcast_to(total[None, :, rows_here:], (ways_row, thin_cols, width))
    diag_grad = jnp.sum(exchange(mine, "row"), axis=0).T
    return (panel_grad, diag_grad)


def solution(mesh):
    in_specs = (P("row", "col"), P("row", "col"), P("row", "col"), P(), P())
    out_specs = (P("row", "col"), P(None, "col"))
    return jax.shard_map(body, mesh=mesh, in_specs=in_specs, out_specs=out_specs, check_vma=False)
```

```python
import jax
import jax.numpy as jnp
from jax import lax
from jax.experimental import pallas as pl
from jax.experimental.pallas import tpu as pltpu
from jax.sharding import PartitionSpec as P

X_WAYS = 4
F32 = jnp.float32


def exchange(value, axis, groups=None):
    return lax.all_to_all(value, axis, split_axis=0, concat_axis=0, axis_index_groups=groups)


def halves(value):
    high = value.astype(jnp.bfloat16)
    low = (value - high.astype(F32)).astype(jnp.bfloat16)
    return high, low


def dot(a, b, contract):
    a_high, a_low = halves(a)
    b_high, b_low = halves(b)

    def one(p, q):
        return lax.dot_general(p, q, (contract, ((), ())), preferred_element_type=F32)

    return one(a_high, b_high) + (one(a_high, b_low) + one(a_low, b_high))


def call(kernel, shapes, *args, scalars=0):
    vmem = pl.BlockSpec(memory_space=pltpu.VMEM)
    smem = pl.BlockSpec(memory_space=pltpu.SMEM)
    single = not isinstance(shapes, (list, tuple))
    outs = [shapes] if single else list(shapes)
    got = pl.pallas_call(
        kernel,
        out_shape=[jax.ShapeDtypeStruct(s, F32) for s in map(tuple, (o.shape for o in outs))],
        in_specs=[smem] * scalars + [vmem] * (len(args) - scalars),
        out_specs=[vmem] * len(outs),
        compiler_params=pltpu.CompilerParams(vmem_limit_bytes=48 << 20),
    )(*args)
    return got[0] if single else got


def like(*shape):
    return jax.ShapeDtypeStruct(shape, F32)


def spread(index_ref, thin_ref, out_ref, *, width, ratio):
    row = lax.axis_index("row")
    ways_row = out_ref.shape[0]
    ways_col = ratio * ways_row
    half = thin_ref.shape[1] // ratio
    for p in range(ratio):
        column = row + p * ways_row
        offset = lax.rem(column + 2048 * ways_col - index_ref[0] - 1, ways_col) // ways_row
        for j in range(half // width):
            at = ratio * j * width
            piece = thin_ref[:, at : at + width]
            for i in range(1, ratio):
                piece = jnp.where(offset == i, thin_ref[:, at + i * width : at + (i + 1) * width], piece)
            for r in range(ways_row):
                out_ref[r, :, p * half + j * width : p * half + (j + 1) * width] = piece


def route(every_ref, thin_ref, out_ref):
    ways_row = every_ref.shape[0]
    ways_col = out_ref.shape[0]
    quarter = thin_ref.shape[1] // X_WAYS
    cols = out_ref.shape[2] - quarter
    for c in range(ways_col):
        p = c // ways_row
        x = c // (ways_col // X_WAYS)
        out_ref[c, :, :cols] = every_ref[c % ways_row, :, p * cols : (p + 1) * cols]
        out_ref[c, :, cols:] = thin_ref[:, x * quarter : (x + 1) * quarter]


def multiply(got_ref, trail_ref, adjoint_ref, inv_ref, out_ref, panel_ref, work_ref):
    ways_col, thin_cols, _ = got_ref.shape
    rows_here, cols = trail_ref.shape
    for c in range(ways_col):
        work_ref[c * thin_cols : (c + 1) * thin_cols, :] = got_ref[c]
    inv = inv_ref[...]
    scaled = dot(inv.T * -2.0, work_ref[:, :cols], ((1,), (0,)))
    panel_ref[...] = work_ref[:, cols:]
    col = lax.axis_index("col")
    mine = inv_ref[pl.ds(col * thin_cols, thin_cols), :].T
    quarter = rows_here // X_WAYS
    for x in range(X_WAYS):
        at = slice(x * quarter, (x + 1) * quarter)
        local = dot(scaled, trail_ref[at, :], ((1,), (1,)))
        for i in range(thin_cols):
            local = local + mine[:, i : i + 1] * adjoint_ref[i : i + 1, at]
        out_ref[x] = local


def gram(parts_ref, panel_ref, out_ref):
    ways_col, thin_cols, _ = out_ref.shape
    total = parts_ref[0]
    for x in range(1, X_WAYS):
        total = total + parts_ref[x]
    quarter = total.shape[1]
    diag = dot(-panel_ref[...], total, ((1,), (1,)))
    for c in range(ways_col):
        at = slice(c * thin_cols, (c + 1) * thin_cols)
        out_ref[c, :, :quarter] = total[at, :]
        out_ref[c, :, quarter:] = diag[at, :]


def finish(parts_ref, grad_ref, out_ref):
    ways_col = parts_ref.shape[0]
    y_ways = ways_col // X_WAYS
    quarter = grad_ref.shape[1] // X_WAYS
    diag = None
    for x in range(X_WAYS):
        total = parts_ref[x * y_ways]
        for y in range(1, y_ways):
            total = total + parts_ref[x * y_ways + y]
        grad_ref[:, x * quarter : (x + 1) * quarter] = total[:, :quarter]
        diag = total[:, quarter:] if diag is None else diag + total[:, quarter:]
    for r in range(out_ref.shape[0]):
        out_ref[r] = diag


def last(parts_ref, out_ref):
    total = parts_ref[0]
    for r in range(1, parts_ref.shape[0]):
        total = total + parts_ref[r]
    out_ref[...] = total


def body(trail_adjoint, panel, panel_adjoint, inv_diag, panel_index):
    rows_here, thin_cols = panel.shape
    width = inv_diag.shape[0]
    ways_row = lax.axis_size("row")
    ways_col = lax.axis_size("col")
    cols = trail_adjoint.shape[1]
    quarter = rows_here // X_WAYS
    y_ways = ways_col // X_WAYS
    groups = [[x * y_ways + y for x in range(X_WAYS)] for y in range(y_ways)]
    thin = panel.T

    def spreading(*refs):
        spread(*refs, width=width, ratio=ways_col // ways_row)

    copies = call(spreading, like(ways_row, thin_cols, rows_here), panel_index, thin, scalars=1)
    sent = call(route, like(ways_col, thin_cols, cols + quarter), exchange(copies, "row"), thin)
    got = exchange(sent, "col")
    vmem = pl.BlockSpec(memory_space=pltpu.VMEM)
    parts, panel_rows = pl.pallas_call(
        multiply,
        out_shape=[like(X_WAYS, width, quarter), like(width, quarter)],
        in_specs=[vmem] * 4,
        out_specs=[vmem] * 2,
        scratch_shapes=[pltpu.VMEM((width, cols + quarter), F32)],
        compiler_params=pltpu.CompilerParams(vmem_limit_bytes=48 << 20),
    )(got, trail_adjoint, panel_adjoint.T, inv_diag)
    both = call(gram, like(ways_col, thin_cols, quarter + width), exchange(parts, "col", groups), panel_rows)
    grad, mine = call(
        finish, [like(thin_cols, rows_here), like(ways_row, thin_cols, width)], exchange(both, "col")
    )
    diag = call(last, like(thin_cols, width), exchange(mine, "row"))
    return (grad.T, diag.T)


def solution(mesh):
    in_specs = (P("row", "col"), P("row", "col"), P("row", "col"), P(), P())
    out_specs = (P("row", "col"), P(None, "col"))
    return jax.shard_map(body, mesh=mesh, in_specs=in_specs, out_specs=out_specs, check_vma=False)
```

```python
import jax
import jax.numpy as jnp
from jax import lax
from jax.experimental import pallas as pl
from jax.experimental.pallas import tpu as pltpu
from jax.sharding import PartitionSpec as P

X_WAYS = 4
CORES = 2
F32 = jnp.float32


def exchange(value, axis, groups=None):
    return lax.all_to_all(value, axis, split_axis=0, concat_axis=0, axis_index_groups=groups)


def halves(value):
    high = value.astype(jnp.bfloat16)
    low = (value - high.astype(F32)).astype(jnp.bfloat16)
    return high, low


def dot(a, b, contract):
    a_high, a_low = halves(a)
    b_high, b_low = halves(b)

    def one(p, q):
        return lax.dot_general(p, q, (contract, ((), ())), preferred_element_type=F32)

    return one(a_high, b_high) + (one(a_high, b_low) + one(a_low, b_high))


def call(kernel, shapes, *args, scalars=0):
    vmem = pl.BlockSpec(memory_space=pltpu.VMEM)
    smem = pl.BlockSpec(memory_space=pltpu.SMEM)
    single = not isinstance(shapes, (list, tuple))
    outs = [shapes] if single else list(shapes)
    got = pl.pallas_call(
        kernel,
        out_shape=[jax.ShapeDtypeStruct(s, F32) for s in map(tuple, (o.shape for o in outs))],
        in_specs=[smem] * scalars + [vmem] * (len(args) - scalars),
        out_specs=[vmem] * len(outs),
        compiler_params=pltpu.CompilerParams(vmem_limit_bytes=48 << 20),
    )(*args)
    return got[0] if single else got


def like(*shape):
    return jax.ShapeDtypeStruct(shape, F32)


def spread(index_ref, thin_ref, out_ref, *, width, ratio):
    row = lax.axis_index("row")
    ways_row = out_ref.shape[0]
    ways_col = ratio * ways_row
    share = out_ref.shape[2] // ratio
    blocks = share // width
    for p in range(ratio):
        column = row + p * ways_row
        offset = lax.rem(column + 2048 * ways_col - index_ref[0] - 1, ways_col) // ways_row
        for j in range(CORES * blocks):
            at = ratio * j * width
            piece = thin_ref[:, at : at + width]
            for i in range(1, ratio):
                piece = jnp.where(offset == i, thin_ref[:, at + i * width : at + (i + 1) * width], piece)
            to = p * share + j % blocks * width
            for r in range(j // blocks, ways_row, CORES):
                out_ref[r, :, to : to + width] = piece


def route(every_ref, thin_ref, out_ref):
    ways_row = every_ref.shape[0]
    ways_col = out_ref.shape[0]
    quarter = thin_ref.shape[1] // X_WAYS
    share = out_ref.shape[2] - quarter
    for c in range(ways_col):
        p = c // ways_row
        x = c // (ways_col // X_WAYS)
        out_ref[c, :, :share] = every_ref[c % ways_row, :, p * share : (p + 1) * share]
        out_ref[c, :, share:] = thin_ref[:, x * quarter : (x + 1) * quarter]


def multiply(pair_ref, got_ref, trail_ref, adjoint_ref, inv_ref, out_ref, panel_ref, work_ref):
    ways_col, thin_cols, _ = got_ref.shape
    rows_here, cols = trail_ref.shape
    share = cols // CORES
    for c in range(ways_col):
        at = slice(c * thin_cols, (c + 1) * thin_cols)
        for core in range(CORES):
            work_ref[at, core * share : (core + 1) * share] = pair_ref[core, c, :, :share]
        panel_ref[at, :] = got_ref[c, :, share:]
    inv = inv_ref[...]
    scaled = dot(inv.T * -2.0, work_ref[...], ((1,), (0,)))
    col = lax.axis_index("col")
    mine = inv_ref[pl.ds(col * thin_cols, thin_cols), :].T
    quarter = rows_here // X_WAYS
    for x in range(X_WAYS):
        at = slice(x * quarter, (x + 1) * quarter)
        local = dot(scaled, trail_ref[at, :], ((1,), (1,)))
        for i in range(thin_cols):
            local = local + mine[:, i : i + 1] * adjoint_ref[i : i + 1, at]
        out_ref[x] = local


def gram(parts_ref, panel_ref, out_ref):
    ways_col, thin_cols, _ = out_ref.shape
    total = parts_ref[0]
    for x in range(1, X_WAYS):
        total = total + parts_ref[x]
    quarter = total.shape[1]
    diag = dot(-panel_ref[...], total, ((1,), (1,)))
    for c in range(ways_col):
        at = slice(c * thin_cols, (c + 1) * thin_cols)
        out_ref[c, :, :quarter] = total[at, :]
        out_ref[c, :, quarter:] = diag[at, :]


def finish(parts_ref, grad_ref, out_ref):
    ways_col = parts_ref.shape[0]
    y_ways = ways_col // X_WAYS
    quarter = grad_ref.shape[1] // X_WAYS
    diag = None
    for x in range(X_WAYS):
        total = parts_ref[x * y_ways]
        for y in range(1, y_ways):
            total = total + parts_ref[x * y_ways + y]
        grad_ref[:, x * quarter : (x + 1) * quarter] = total[:, :quarter]
        diag = total[:, quarter:] if diag is None else diag + total[:, quarter:]
    for r in range(out_ref.shape[0]):
        out_ref[r] = diag


def last(parts_ref, out_ref):
    total = parts_ref[0]
    for r in range(1, parts_ref.shape[0]):
        total = total + parts_ref[r]
    out_ref[...] = total


def body(trail_adjoint, panel, panel_adjoint, inv_diag, panel_index):
    rows_here, thin_cols = panel.shape
    width = inv_diag.shape[0]
    ways_row = lax.axis_size("row")
    ways_col = lax.axis_size("col")
    cols = trail_adjoint.shape[1]
    quarter = rows_here // X_WAYS
    y_ways = ways_col // X_WAYS
    groups = [[x * y_ways + y for x in range(X_WAYS)] for y in range(y_ways)]
    thin = panel.T

    def spreading(*refs):
        spread(*refs, width=width, ratio=ways_col // ways_row)

    share = cols // CORES
    copies = call(spreading, like(ways_row, thin_cols, rows_here // CORES), panel_index, thin, scalars=1)
    sent = call(route, like(ways_col, thin_cols, share + quarter), exchange(copies, "row"), thin)
    got = exchange(sent, "col")
    chips = [list(range(r, r + CORES)) for r in range(0, ways_row, CORES)]
    pair = lax.all_gather(got, "row", axis=0, axis_index_groups=chips)
    vmem = pl.BlockSpec(memory_space=pltpu.VMEM)
    parts, panel_rows = pl.pallas_call(
        multiply,
        out_shape=[like(X_WAYS, width, quarter), like(width, quarter)],
        in_specs=[vmem] * 5,
        out_specs=[vmem] * 2,
        scratch_shapes=[pltpu.VMEM((width, cols), F32)],
        compiler_params=pltpu.CompilerParams(vmem_limit_bytes=48 << 20),
    )(pair, got, trail_adjoint, panel_adjoint.T, inv_diag)
    both = call(gram, like(ways_col, thin_cols, quarter + width), exchange(parts, "col", groups), panel_rows)
    grad, mine = call(
        finish, [like(thin_cols, rows_here), like(ways_row, thin_cols, width)], exchange(both, "col")
    )
    diag = call(last, like(thin_cols, width), exchange(mine, "row"))
    return (grad.T, diag.T)


def solution(mesh):
    in_specs = (P("row", "col"), P("row", "col"), P("row", "col"), P(), P())
    out_specs = (P("row", "col"), P(None, "col"))
    return jax.shard_map(body, mesh=mesh, in_specs=in_specs, out_specs=out_specs, check_vma=False)
```

```python
import jax
import jax.numpy as jnp
from jax import lax
from jax.experimental import pallas as pl
from jax.experimental.pallas import tpu as pltpu
from jax.sharding import PartitionSpec as P

X_WAYS = 4
CORES = 2
F32 = jnp.float32


def exchange(value, axis, groups=None):
    return lax.all_to_all(value, axis, split_axis=0, concat_axis=0, axis_index_groups=groups)


def halves(value):
    high = value.astype(jnp.bfloat16)
    low = (value - high.astype(F32)).astype(jnp.bfloat16)
    return high, low


def dot(a, b, contract):
    a_high, a_low = halves(a)
    b_high, b_low = halves(b)

    def one(p, q):
        return lax.dot_general(p, q, (contract, ((), ())), preferred_element_type=F32)

    return one(a_high, b_high) + (one(a_high, b_low) + one(a_low, b_high))


def call(kernel, shapes, *args, scalars=0):
    vmem = pl.BlockSpec(memory_space=pltpu.VMEM)
    smem = pl.BlockSpec(memory_space=pltpu.SMEM)
    single = not isinstance(shapes, (list, tuple))
    outs = [shapes] if single else list(shapes)
    got = pl.pallas_call(
        kernel,
        out_shape=[jax.ShapeDtypeStruct(s, F32) for s in map(tuple, (o.shape for o in outs))],
        in_specs=[smem] * scalars + [vmem] * (len(args) - scalars),
        out_specs=[vmem] * len(outs),
        compiler_params=pltpu.CompilerParams(vmem_limit_bytes=48 << 20),
    )(*args)
    return got[0] if single else got


def like(*shape):
    return jax.ShapeDtypeStruct(shape, F32)


def spread(index_ref, thin_ref, out_ref, *, width, ratio):
    row = lax.axis_index("row")
    ways_row = out_ref.shape[0]
    ways_col = ratio * ways_row
    share = out_ref.shape[2] // ratio
    blocks = share // width
    for p in range(ratio):
        column = row + p * ways_row
        offset = lax.rem(column + 2048 * ways_col - index_ref[0] - 1, ways_col) // ways_row
        for j in range(CORES * blocks):
            at = ratio * j * width
            piece = thin_ref[:, at : at + width]
            for i in range(1, ratio):
                piece = jnp.where(offset == i, thin_ref[:, at + i * width : at + (i + 1) * width], piece)
            to = p * share + j % blocks * width
            for r in range(j // blocks, ways_row, CORES):
                out_ref[r, :, to : to + width] = piece


def route(every_ref, thin_ref, out_ref):
    ways_row = every_ref.shape[0]
    ways_col = out_ref.shape[0]
    quarter = thin_ref.shape[1] // X_WAYS
    share = out_ref.shape[2] - quarter
    for c in range(ways_col):
        p = c // ways_row
        x = c // (ways_col // X_WAYS)
        out_ref[c, :, :share] = every_ref[c % ways_row, :, p * share : (p + 1) * share]
        out_ref[c, :, share:] = thin_ref[:, x * quarter : (x + 1) * quarter]


def multiply(pair_ref, got_ref, trail_ref, adjoint_ref, out_ref, panel_ref, work_ref):
    ways_col, thin_cols, _ = got_ref.shape
    rows_here, cols = trail_ref.shape
    share = cols // CORES
    for c in range(ways_col):
        at = slice(c * thin_cols, (c + 1) * thin_cols)
        for core in range(CORES):
            work_ref[at, core * share : (core + 1) * share] = pair_ref[core, c, :, :share]
        panel_ref[at, :] = got_ref[c, :, share:]
    scaled = work_ref[...] * -2.0
    per_eight = 8 // thin_cols
    col = lax.axis_index("col")
    eight = pl.ds(pl.multiple_of(col // per_eight * 8, 8), 8)
    owner = lax.broadcasted_iota(jnp.int32, (8, rows_here // X_WAYS), 0) // thin_cols
    quarter = rows_here // X_WAYS
    for x in range(X_WAYS):
        at = slice(x * quarter, (x + 1) * quarter)
        out_ref[x] = dot(scaled, trail_ref[at, :], ((1,), (1,)))
        added = jnp.concatenate([adjoint_ref[:, at]] * per_eight, axis=0)
        added = jnp.where(owner == lax.rem(col, per_eight), added, jnp.zeros_like(added))
        out_ref[x, eight, :] = out_ref[x, eight, :] + added


def gram(parts_ref, panel_ref, inv_ref, out_ref):
    ways_col, thin_cols, _ = out_ref.shape
    total = parts_ref[0]
    for x in range(1, X_WAYS):
        total = total + parts_ref[x]
    total = dot(inv_ref[...].T, total, ((1,), (0,)))
    quarter = total.shape[1]
    diag = dot(-panel_ref[...], total, ((1,), (1,)))
    for c in range(ways_col):
        at = slice(c * thin_cols, (c + 1) * thin_cols)
        out_ref[c, :, :quarter] = total[at, :]
        out_ref[c, :, quarter:] = diag[at, :]


def finish(parts_ref, grad_ref, out_ref):
    ways_col = parts_ref.shape[0]
    y_ways = ways_col // X_WAYS
    quarter = grad_ref.shape[1] // X_WAYS
    diag = None
    for x in range(X_WAYS):
        total = parts_ref[x * y_ways]
        for y in range(1, y_ways):
            total = total + parts_ref[x * y_ways + y]
        grad_ref[:, x * quarter : (x + 1) * quarter] = total[:, :quarter]
        diag = total[:, quarter:] if diag is None else diag + total[:, quarter:]
    for r in range(out_ref.shape[0]):
        out_ref[r] = diag


def last(parts_ref, grad_ref, out_ref, grad_out_ref):
    grad_out_ref[...] = grad_ref[...]
    total = parts_ref[0]
    for r in range(1, parts_ref.shape[0]):
        total = total + parts_ref[r]
    out_ref[...] = total


def body(trail_adjoint, panel, panel_adjoint, inv_diag, panel_index):
    rows_here, thin_cols = panel.shape
    width = inv_diag.shape[0]
    ways_row = lax.axis_size("row")
    ways_col = lax.axis_size("col")
    cols = trail_adjoint.shape[1]
    quarter = rows_here // X_WAYS
    y_ways = ways_col // X_WAYS
    groups = [[x * y_ways + y for x in range(X_WAYS)] for y in range(y_ways)]
    thin = panel.T

    def spreading(*refs):
        spread(*refs, width=width, ratio=ways_col // ways_row)

    share = cols // CORES
    copies = call(spreading, like(ways_row, thin_cols, rows_here // CORES), panel_index, thin, scalars=1)
    sent = call(route, like(ways_col, thin_cols, share + quarter), exchange(copies, "row"), thin)
    got = exchange(sent, "col")
    chips = [list(range(r, r + CORES)) for r in range(0, ways_row, CORES)]
    pair = lax.all_gather(got, "row", axis=0, axis_index_groups=chips)
    vmem = pl.BlockSpec(memory_space=pltpu.VMEM)
    parts, panel_rows = pl.pallas_call(
        multiply,
        out_shape=[like(X_WAYS, width, quarter), like(width, quarter)],
        in_specs=[vmem] * 4,
        out_specs=[vmem] * 2,
        scratch_shapes=[pltpu.VMEM((width, cols), F32)],
        compiler_params=pltpu.CompilerParams(vmem_limit_bytes=48 << 20),
    )(pair, got, trail_adjoint, panel_adjoint.T)
    both = call(gram, like(ways_col, thin_cols, quarter + width), exchange(parts, "col", groups), panel_rows, inv_diag)
    grad, mine = call(
        finish, [like(thin_cols, rows_here), like(ways_row, thin_cols, width)], exchange(both, "col")
    )
    diag, grad = call(last, [like(thin_cols, width), like(thin_cols, rows_here)], exchange(mine, "row"), grad)
    return (grad.T, diag.T)


def solution(mesh):
    in_specs = (P("row", "col"), P("row", "col"), P("row", "col"), P(), P())
    out_specs = (P("row", "col"), P(None, "col"))
    return jax.shard_map(body, mesh=mesh, in_specs=in_specs, out_specs=out_specs, check_vma=False)
```

```python
import jax
import jax.numpy as jnp
from jax import lax
from jax.experimental import pallas as pl
from jax.experimental.pallas import tpu as pltpu
from jax.sharding import PartitionSpec as P

Y_WAYS = 8
BLOCK_X, BLOCK_Y = 4, 2
BLOCK = BLOCK_X * BLOCK_Y
CORES = 2
F32 = jnp.float32


def place(col):
    x, y = col // Y_WAYS, col % Y_WAYS
    return x % BLOCK_X * BLOCK_Y + y % BLOCK_Y


def exchange(value, axis, groups=None):
    return lax.all_to_all(value, axis, split_axis=0, concat_axis=0, axis_index_groups=groups)


def halves(value):
    high = value.astype(jnp.bfloat16)
    low = (value - high.astype(F32)).astype(jnp.bfloat16)
    return high, low


def dot(a, b, contract):
    a_high, a_low = halves(a)
    b_high, b_low = halves(b)

    def one(p, q):
        return lax.dot_general(p, q, (contract, ((), ())), preferred_element_type=F32)

    return one(a_high, b_high) + (one(a_high, b_low) + one(a_low, b_high))


def call(kernel, shapes, *args, scalars=0):
    vmem = pl.BlockSpec(memory_space=pltpu.VMEM)
    smem = pl.BlockSpec(memory_space=pltpu.SMEM)
    single = not isinstance(shapes, (list, tuple))
    outs = [shapes] if single else list(shapes)
    got = pl.pallas_call(
        kernel,
        out_shape=[jax.ShapeDtypeStruct(s, F32) for s in map(tuple, (o.shape for o in outs))],
        in_specs=[smem] * scalars + [vmem] * (len(args) - scalars),
        out_specs=[vmem] * len(outs),
        compiler_params=pltpu.CompilerParams(vmem_limit_bytes=48 << 20),
    )(*args)
    return got[0] if single else got


def like(*shape):
    return jax.ShapeDtypeStruct(shape, F32)


def spread(index_ref, thin_ref, out_ref, *, width, ratio):
    row = lax.axis_index("row")
    ways_row = out_ref.shape[0]
    ways_col = ratio * ways_row
    share = out_ref.shape[2] // ratio
    blocks = share // width
    for p in range(ratio):
        column = row + p * ways_row
        offset = lax.rem(column + 2048 * ways_col - index_ref[0] - 1, ways_col) // ways_row
        for j in range(CORES * blocks):
            at = ratio * j * width
            piece = thin_ref[:, at : at + width]
            for i in range(1, ratio):
                piece = jnp.where(offset == i, thin_ref[:, at + i * width : at + (i + 1) * width], piece)
            to = p * share + j % blocks * width
            for r in range(j // blocks, ways_row, CORES):
                out_ref[r, :, to : to + width] = piece


def route(every_ref, thin_ref, out_ref):
    ways_row = every_ref.shape[0]
    ways_col = out_ref.shape[0]
    part = thin_ref.shape[1] // BLOCK
    share = out_ref.shape[2] - part
    for c in range(ways_col):
        p = c // ways_row
        x = place(c)
        out_ref[c, :, :share] = every_ref[c % ways_row, :, p * share : (p + 1) * share]
        out_ref[c, :, share:] = thin_ref[:, x * part : (x + 1) * part]


def multiply(pair_ref, got_ref, trail_ref, adjoint_ref, out_ref, panel_ref, work_ref):
    ways_col, thin_cols, _ = got_ref.shape
    rows_here, cols = trail_ref.shape
    share = cols // CORES
    for c in range(ways_col):
        at = slice(c * thin_cols, (c + 1) * thin_cols)
        for core in range(CORES):
            work_ref[at, core * share : (core + 1) * share] = pair_ref[core, c, :, :share]
        panel_ref[at, :] = got_ref[c, :, share:]
    scaled = work_ref[...] * -2.0
    per_eight = 8 // thin_cols
    col = lax.axis_index("col")
    eight = pl.ds(pl.multiple_of(col // per_eight * 8, 8), 8)
    owner = lax.broadcasted_iota(jnp.int32, (8, rows_here // BLOCK), 0) // thin_cols
    part = rows_here // BLOCK
    for x in range(BLOCK):
        at = slice(x * part, (x + 1) * part)
        out_ref[x] = dot(scaled, trail_ref[at, :], ((1,), (1,)))
        added = jnp.concatenate([adjoint_ref[:, at]] * per_eight, axis=0)
        added = jnp.where(owner == lax.rem(col, per_eight), added, jnp.zeros_like(added))
        out_ref[x, eight, :] = out_ref[x, eight, :] + added


def gram(parts_ref, panel_ref, inv_ref, out_ref):
    ways_col, thin_cols, _ = out_ref.shape
    total = parts_ref[0]
    for x in range(1, BLOCK):
        total = total + parts_ref[x]
    total = dot(inv_ref[...].T, total, ((1,), (0,)))
    part = total.shape[1]
    diag = dot(-panel_ref[...], total, ((1,), (1,)))
    for c in range(ways_col):
        at = slice(c * thin_cols, (c + 1) * thin_cols)
        out_ref[c, :, :part] = total[at, :]
        out_ref[c, :, part:] = diag[at, :]


def finish(parts_ref, grad_ref, out_ref):
    ways_col = parts_ref.shape[0]
    part = grad_ref.shape[1] // BLOCK
    diag = None
    for i in range(BLOCK):
        total = None
        for c in range(ways_col):
            if place(c) == i:
                total = parts_ref[c] if total is None else total + parts_ref[c]
        grad_ref[:, i * part : (i + 1) * part] = total[:, :part]
        diag = total[:, part:] if diag is None else diag + total[:, part:]
    for r in range(out_ref.shape[0]):
        out_ref[r] = diag


def last(parts_ref, grad_ref, out_ref, grad_out_ref):
    grad_out_ref[...] = grad_ref[...]
    total = parts_ref[0]
    for r in range(1, parts_ref.shape[0]):
        total = total + parts_ref[r]
    out_ref[...] = total


def body(trail_adjoint, panel, panel_adjoint, inv_diag, panel_index):
    rows_here, thin_cols = panel.shape
    width = inv_diag.shape[0]
    ways_row = lax.axis_size("row")
    ways_col = lax.axis_size("col")
    cols = trail_adjoint.shape[1]
    part = rows_here // BLOCK
    groups = {}
    for c in range(ways_col):
        block = (c // Y_WAYS // BLOCK_X, c % Y_WAYS // BLOCK_Y)
        groups.setdefault(block, []).append(c)
    groups = [sorted(g, key=place) for g in groups.values()]
    thin = panel.T

    def spreading(*refs):
        spread(*refs, width=width, ratio=ways_col // ways_row)

    share = cols // CORES
    copies = call(spreading, like(ways_row, thin_cols, rows_here // CORES), panel_index, thin, scalars=1)
    sent = call(route, like(ways_col, thin_cols, share + part), exchange(copies, "row"), thin)
    got = exchange(sent, "col")
    chips = [list(range(r, r + CORES)) for r in range(0, ways_row, CORES)]
    pair = lax.all_gather(jnp.concatenate([got, got[:, :, :128]], axis=2), "row", axis=0, axis_index_groups=chips)
    vmem = pl.BlockSpec(memory_space=pltpu.VMEM)
    parts, panel_rows = pl.pallas_call(
        multiply,
        out_shape=[like(BLOCK, width, part), like(width, part)],
        in_specs=[vmem] * 4,
        out_specs=[vmem] * 2,
        scratch_shapes=[pltpu.VMEM((width, cols), F32)],
        compiler_params=pltpu.CompilerParams(vmem_limit_bytes=48 << 20),
    )(pair, got, trail_adjoint, panel_adjoint.T)
    both = call(gram, like(ways_col, thin_cols, part + width), exchange(parts, "col", groups), panel_rows, inv_diag)
    grad, mine = call(
        finish, [like(thin_cols, rows_here), like(ways_row, thin_cols, width)], exchange(both, "col")
    )
    diag, grad = call(last, [like(thin_cols, width), like(thin_cols, rows_here)], exchange(mine, "row"), grad)
    return (grad.T, diag.T)


def solution(mesh):
    in_specs = (P("row", "col"), P("row", "col"), P("row", "col"), P(), P())
    out_specs = (P("row", "col"), P(None, "col"))
    return jax.shard_map(body, mesh=mesh, in_specs=in_specs, out_specs=out_specs, check_vma=False)
```

```python
import jax
import jax.numpy as jnp
from jax import lax
from jax.experimental import pallas as pl
from jax.experimental.pallas import tpu as pltpu
from jax.sharding import PartitionSpec as P

Y_WAYS = 8
BLOCK_X, BLOCK_Y = 4, 2
BLOCK = BLOCK_X * BLOCK_Y
CORES = 2
F32 = jnp.float32


def order(ways):
    stride = 5 if ways > 16 else 5
    return [stride * i % ways for i in range(ways)]


def place(col):
    x, y = col // Y_WAYS, col % Y_WAYS
    return x % BLOCK_X * BLOCK_Y + y % BLOCK_Y


def exchange(value, axis, groups=None):
    return lax.all_to_all(value, axis, split_axis=0, concat_axis=0, axis_index_groups=groups)


def halves(value):
    high = value.astype(jnp.bfloat16)
    low = (value - high.astype(F32)).astype(jnp.bfloat16)
    return high, low


def dot(a, b, contract):
    a_high, a_low = halves(a)
    b_high, b_low = halves(b)

    def one(p, q):
        return lax.dot_general(p, q, (contract, ((), ())), preferred_element_type=F32)

    rows = a.shape[0]
    both = one(jnp.concatenate([a_high, a_low], axis=0), b_high)
    return both[:rows] + (one(a_high, b_low) + both[rows:])


def call(kernel, shapes, *args, scalars=0):
    vmem = pl.BlockSpec(memory_space=pltpu.VMEM)
    smem = pl.BlockSpec(memory_space=pltpu.SMEM)
    single = not isinstance(shapes, (list, tuple))
    outs = [shapes] if single else list(shapes)
    got = pl.pallas_call(
        kernel,
        out_shape=[jax.ShapeDtypeStruct(s, F32) for s in map(tuple, (o.shape for o in outs))],
        in_specs=[smem] * scalars + [vmem] * (len(args) - scalars),
        out_specs=[vmem] * len(outs),
        compiler_params=pltpu.CompilerParams(vmem_limit_bytes=48 << 20),
    )(*args)
    return got[0] if single else got


def like(*shape):
    return jax.ShapeDtypeStruct(shape, F32)


def spread(index_ref, thin_ref, out_ref, *, width, ratio):
    row = lax.axis_index("row")
    ways_row = out_ref.shape[0]
    ways_col = ratio * ways_row
    share = out_ref.shape[2] // ratio
    blocks = share // width
    for p in range(ratio):
        column = row + p * ways_row
        offset = lax.rem(column + 2048 * ways_col - index_ref[0] - 1, ways_col) // ways_row
        for j in range(CORES * blocks):
            at = ratio * j * width
            piece = thin_ref[:, at : at + width]
            for i in range(1, ratio):
                piece = jnp.where(offset == i, thin_ref[:, at + i * width : at + (i + 1) * width], piece)
            to = p * share + j % blocks * width
            for i, r in enumerate(order(ways_row)):
                if r % CORES == j // blocks:
                    out_ref[i, :, to : to + width] = piece


def route(every_ref, thin_ref, out_ref):
    ways_row = every_ref.shape[0]
    ways_col = out_ref.shape[0]
    part = thin_ref.shape[1] // BLOCK
    share = out_ref.shape[2] - part
    for i, c in enumerate(order(ways_col)):
        p = c // ways_row
        source = order(ways_row).index(c % ways_row)
        x = place(c)
        out_ref[i, :, :share] = every_ref[source, :, p * share : (p + 1) * share]
        out_ref[i, :, share:] = thin_ref[:, x * part : (x + 1) * part]


def multiply(pair_ref, got_ref, trail_ref, adjoint_ref, out_ref, panel_ref, work_ref):
    ways_col, thin_cols, _ = got_ref.shape
    rows_here, cols = trail_ref.shape
    share = cols // CORES
    for i, c in enumerate(order(ways_col)):
        at = slice(c * thin_cols, (c + 1) * thin_cols)
        for core in range(CORES):
            work_ref[at, core * share : (core + 1) * share] = pair_ref[core, i, :, :share]
        panel_ref[at, :] = got_ref[i, :, share:]
    scaled = work_ref[...] * -2.0
    per_eight = 8 // thin_cols
    col = lax.axis_index("col")
    eight = pl.ds(pl.multiple_of(col // per_eight * 8, 8), 8)
    owner = lax.broadcasted_iota(jnp.int32, (8, rows_here // BLOCK), 0) // thin_cols
    part = rows_here // BLOCK
    product = dot(scaled, trail_ref[...], ((1,), (1,)))
    for x in range(BLOCK):
        at = slice(x * part, (x + 1) * part)
        out_ref[x] = product[:, at]
        added = jnp.concatenate([adjoint_ref[:, at]] * per_eight, axis=0)
        added = jnp.where(owner == lax.rem(col, per_eight), added, jnp.zeros_like(added))
        out_ref[x, eight, :] = out_ref[x, eight, :] + added


def gram(parts_ref, panel_ref, inv_ref, out_ref):
    ways_col, thin_cols, _ = out_ref.shape
    total = parts_ref[0]
    for x in range(1, BLOCK):
        total = total + parts_ref[x]
    total = dot(inv_ref[...].T, total, ((1,), (0,)))
    part = total.shape[1]
    diag = dot(-panel_ref[...], total, ((1,), (1,)))
    for i, c in enumerate(order(ways_col)):
        at = slice(c * thin_cols, (c + 1) * thin_cols)
        out_ref[i, :, :part] = total[at, :]
        out_ref[i, :, part:] = diag[at, :]


def finish(parts_ref, grad_ref, out_ref):
    ways_col = parts_ref.shape[0]
    part = grad_ref.shape[1] // BLOCK
    diag = None
    for i in range(BLOCK):
        total = None
        for j, c in enumerate(order(ways_col)):
            if place(c) == i:
                total = parts_ref[j] if total is None else total + parts_ref[j]
        grad_ref[:, i * part : (i + 1) * part] = total[:, :part]
        diag = total[:, part:] if diag is None else diag + total[:, part:]
    for r in range(out_ref.shape[0]):
        out_ref[r] = diag


def last(parts_ref, grad_ref, out_ref, grad_out_ref):
    grad_out_ref[...] = grad_ref[...]
    total = parts_ref[0]
    for r in range(1, parts_ref.shape[0]):
        total = total + parts_ref[r]
    out_ref[...] = total


def body(trail_adjoint, panel, panel_adjoint, inv_diag, panel_index):
    rows_here, thin_cols = panel.shape
    width = inv_diag.shape[0]
    ways_row = lax.axis_size("row")
    ways_col = lax.axis_size("col")
    cols = trail_adjoint.shape[1]
    part = rows_here // BLOCK
    rows, columns = [order(ways_row)], [order(ways_col)]
    groups = {}
    for c in range(ways_col):
        block = (c // Y_WAYS // BLOCK_X, c % Y_WAYS // BLOCK_Y)
        groups.setdefault(block, []).append(c)
    groups = [sorted(g, key=place) for g in groups.values()]
    thin = panel.T

    def spreading(*refs):
        spread(*refs, width=width, ratio=ways_col // ways_row)

    share = cols // CORES
    copies = call(spreading, like(ways_row, thin_cols, rows_here // CORES), panel_index, thin, scalars=1)
    sent = call(route, like(ways_col, thin_cols, share + part), exchange(copies, "row", rows), thin)
    got = exchange(sent, "col", columns)
    chips = [list(range(r, r + CORES)) for r in range(0, ways_row, CORES)]
    pair = lax.all_gather(jnp.concatenate([got, got[:, :, :128]], axis=2), "row", axis=0, axis_index_groups=chips)
    vmem = pl.BlockSpec(memory_space=pltpu.VMEM)
    parts, panel_rows = pl.pallas_call(
        multiply,
        out_shape=[like(BLOCK, width, part), like(width, part)],
        in_specs=[vmem] * 4,
        out_specs=[vmem] * 2,
        scratch_shapes=[pltpu.VMEM((width, cols), F32)],
        compiler_params=pltpu.CompilerParams(vmem_limit_bytes=48 << 20),
    )(pair, got, trail_adjoint, panel_adjoint.T)
    both = call(gram, like(ways_col, thin_cols, part + width), exchange(parts, "col", groups), panel_rows, inv_diag)
    grad, mine = call(
        finish, [like(thin_cols, rows_here), like(ways_row, thin_cols, width)], exchange(both, "col", columns)
    )
    diag, grad = call(last, [like(thin_cols, width), like(thin_cols, rows_here)], exchange(mine, "row", rows), grad)
    return (grad.T, diag.T)


def solution(mesh):
    in_specs = (P("row", "col"), P("row", "col"), P("row", "col"), P(), P())
    out_specs = (P("row", "col"), P(None, "col"))
    return jax.shard_map(body, mesh=mesh, in_specs=in_specs, out_specs=out_specs, check_vma=False)
```

```python
import jax
import jax.numpy as jnp
from jax import lax
from jax.experimental import pallas as pl
from jax.experimental.pallas import tpu as pltpu
from jax.sharding import PartitionSpec as P

Y_WAYS = 8
BLOCK_X, BLOCK_Y = 4, 2
BLOCK = BLOCK_X * BLOCK_Y
CORES = 2
F32 = jnp.float32


def order(ways):
    stride = 5 if ways > 16 else 5
    return [stride * i % ways for i in range(ways)]


def place(col):
    x, y = col // Y_WAYS, col % Y_WAYS
    return y % BLOCK_Y * BLOCK_X + x % BLOCK_X


def exchange(value, axis, groups=None):
    return lax.all_to_all(value, axis, split_axis=0, concat_axis=0, axis_index_groups=groups)


def halves(value):
    high = value.astype(jnp.bfloat16)
    low = (value - high.astype(F32)).astype(jnp.bfloat16)
    return high, low


def dot(a, b, contract):
    a_high, a_low = halves(a)
    b_high, b_low = halves(b)

    def one(p, q):
        return lax.dot_general(p, q, (contract, ((), ())), preferred_element_type=F32)

    rows = a.shape[0]
    both = one(jnp.concatenate([a_high, a_low], axis=0), b_high)
    return both[:rows] + (one(a_high, b_low) + both[rows:])


def call(kernel, shapes, *args, scalars=0):
    vmem = pl.BlockSpec(memory_space=pltpu.VMEM)
    smem = pl.BlockSpec(memory_space=pltpu.SMEM)
    single = not isinstance(shapes, (list, tuple))
    outs = [shapes] if single else list(shapes)
    got = pl.pallas_call(
        kernel,
        out_shape=[jax.ShapeDtypeStruct(s, F32) for s in map(tuple, (o.shape for o in outs))],
        in_specs=[smem] * scalars + [vmem] * (len(args) - scalars),
        out_specs=[vmem] * len(outs),
        compiler_params=pltpu.CompilerParams(vmem_limit_bytes=48 << 20),
    )(*args)
    return got[0] if single else got


def like(*shape):
    return jax.ShapeDtypeStruct(shape, F32)


def spread(index_ref, thin_ref, out_ref, *, width, ratio):
    row = lax.axis_index("row")
    ways_row = out_ref.shape[0]
    ways_col = ratio * ways_row
    share = out_ref.shape[2] // ratio
    blocks = share // width
    for p in range(ratio):
        column = row + p * ways_row
        offset = lax.rem(column + 2048 * ways_col - index_ref[0] - 1, ways_col) // ways_row
        for j in range(CORES * blocks):
            at = ratio * j * width
            piece = thin_ref[:, at : at + width]
            for i in range(1, ratio):
                piece = jnp.where(offset == i, thin_ref[:, at + i * width : at + (i + 1) * width], piece)
            to = p * share + j % blocks * width
            for i, r in enumerate(order(ways_row)):
                if r % CORES == j // blocks:
                    out_ref[i, :, to : to + width] = piece


def route(every_ref, thin_ref, out_ref):
    ways_row = every_ref.shape[0]
    ways_col = out_ref.shape[0]
    part = thin_ref.shape[1] // BLOCK
    share = out_ref.shape[2] - part
    for i, c in enumerate(order(ways_col)):
        p = c // ways_row
        source = order(ways_row).index(c % ways_row)
        x = place(c)
        out_ref[i, :, :share] = every_ref[source, :, p * share : (p + 1) * share]
        out_ref[i, :, share:] = thin_ref[:, x * part : (x + 1) * part]


def multiply(pair_ref, got_ref, trail_ref, adjoint_ref, out_ref, panel_ref, work_ref):
    ways_col, thin_cols, _ = got_ref.shape
    rows_here, cols = trail_ref.shape
    share = cols // CORES
    for i, c in enumerate(order(ways_col)):
        at = slice(c * thin_cols, (c + 1) * thin_cols)
        for core in range(CORES):
            work_ref[at, core * share : (core + 1) * share] = pair_ref[core, i, :, :share]
        panel_ref[at, :] = got_ref[i, :, share:]
    scaled = work_ref[...] * -2.0
    per_eight = 8 // thin_cols
    col = lax.axis_index("col")
    eight = pl.ds(pl.multiple_of(col // per_eight * 8, 8), 8)
    owner = lax.broadcasted_iota(jnp.int32, (8, rows_here // BLOCK), 0) // thin_cols
    part = rows_here // BLOCK
    product = dot(scaled, trail_ref[...], ((1,), (1,)))
    for x in range(BLOCK):
        at = slice(x * part, (x + 1) * part)
        out_ref[x] = product[:, at]
        added = jnp.concatenate([adjoint_ref[:, at]] * per_eight, axis=0)
        added = jnp.where(owner == lax.rem(col, per_eight), added, jnp.zeros_like(added))
        out_ref[x, eight, :] = out_ref[x, eight, :] + added


def gram(parts_ref, panel_ref, inv_ref, out_ref):
    ways_col, thin_cols, _ = out_ref.shape
    total = parts_ref[0]
    for x in range(1, BLOCK):
        total = total + parts_ref[x]
    total = dot(inv_ref[...].T, total, ((1,), (0,)))
    part = total.shape[1]
    diag = dot(-panel_ref[...], total, ((1,), (1,)))
    for i, c in enumerate(order(ways_col)):
        at = slice(c * thin_cols, (c + 1) * thin_cols)
        out_ref[i, :, :part] = total[at, :]
        out_ref[i, :, part:] = diag[at, :]


def finish(parts_ref, grad_ref, out_ref):
    ways_col = parts_ref.shape[0]
    part = grad_ref.shape[1] // BLOCK
    diag = None
    for i in range(BLOCK):
        total = None
        for j, c in enumerate(order(ways_col)):
            if place(c) == i:
                total = parts_ref[j] if total is None else total + parts_ref[j]
        grad_ref[:, i * part : (i + 1) * part] = total[:, :part]
        diag = total[:, part:] if diag is None else diag + total[:, part:]
    for r in range(out_ref.shape[0]):
        out_ref[r] = diag


def last(parts_ref, grad_ref, out_ref, grad_out_ref):
    grad_out_ref[...] = grad_ref[...]
    total = parts_ref[0]
    for r in range(1, parts_ref.shape[0]):
        total = total + parts_ref[r]
    out_ref[...] = total


def body(trail_adjoint, panel, panel_adjoint, inv_diag, panel_index):
    rows_here, thin_cols = panel.shape
    width = inv_diag.shape[0]
    ways_row = lax.axis_size("row")
    ways_col = lax.axis_size("col")
    cols = trail_adjoint.shape[1]
    part = rows_here // BLOCK
    rows, columns = [order(ways_row)], [order(ways_col)]
    groups = {}
    for c in range(ways_col):
        block = (c // Y_WAYS // BLOCK_X, c % Y_WAYS // BLOCK_Y)
        groups.setdefault(block, []).append(c)
    groups = [sorted(g, key=place) for g in groups.values()]
    thin = panel.T

    def spreading(*refs):
        spread(*refs, width=width, ratio=ways_col // ways_row)

    share = cols // CORES
    copies = call(spreading, like(ways_row, thin_cols, rows_here // CORES), panel_index, thin, scalars=1)
    sent = call(route, like(ways_col, thin_cols, share + part), exchange(copies, "row", rows), thin)
    got = exchange(sent, "col", columns)
    chips = [list(range(r, r + CORES)) for r in range(0, ways_row, CORES)]
    pair = lax.all_gather(jnp.concatenate([got, got[:, :, :128]], axis=2), "row", axis=0, axis_index_groups=chips)
    vmem = pl.BlockSpec(memory_space=pltpu.VMEM)
    parts, panel_rows = pl.pallas_call(
        multiply,
        out_shape=[like(BLOCK, width, part), like(width, part)],
        in_specs=[vmem] * 4,
        out_specs=[vmem] * 2,
        scratch_shapes=[pltpu.VMEM((width, cols), F32)],
        compiler_params=pltpu.CompilerParams(vmem_limit_bytes=48 << 20),
    )(pair, got, trail_adjoint, panel_adjoint.T)
    both = call(gram, like(ways_col, thin_cols, part + width), exchange(parts, "col", groups), panel_rows, inv_diag)
    grad, mine = call(
        finish, [like(thin_cols, rows_here), like(ways_row, thin_cols, width)], exchange(both, "col", columns)
    )
    diag, grad = call(last, [like(thin_cols, width), like(thin_cols, rows_here)], exchange(mine, "row", rows), grad)
    return (grad.T, diag.T)


def solution(mesh):
    in_specs = (P("row", "col"), P("row", "col"), P("row", "col"), P(), P())
    out_specs = (P("row", "col"), P(None, "col"))
    return jax.shard_map(body, mesh=mesh, in_specs=in_specs, out_specs=out_specs, check_vma=False)
```

```python
import jax
import jax.numpy as jnp
from jax import lax
from jax.experimental import pallas as pl
from jax.experimental.pallas import tpu as pltpu
from jax.sharding import PartitionSpec as P

Y_WAYS = 8
BLOCK_X, BLOCK_Y = 4, 2
BLOCK = BLOCK_X * BLOCK_Y
CORES = 2
F32 = jnp.float32


def order(ways):
    stride = 5 if ways > 16 else 3
    return [stride * i % ways for i in range(ways)]


def place(col):
    x, y = col // Y_WAYS, col % Y_WAYS
    return y % BLOCK_Y * BLOCK_X + x % BLOCK_X


def exchange(value, axis, groups=None):
    return lax.all_to_all(value, axis, split_axis=0, concat_axis=0, axis_index_groups=groups)


def halves(value):
    high = value.astype(jnp.bfloat16)
    low = (value - high.astype(F32)).astype(jnp.bfloat16)
    return high, low


def dot(a, b, contract):
    a_high, a_low = halves(a)
    b_high, b_low = halves(b)

    def one(p, q):
        return lax.dot_general(p, q, (contract, ((), ())), preferred_element_type=F32)

    rows = a.shape[0]
    both = one(jnp.concatenate([a_high, a_low], axis=0), b_high)
    return both[:rows] + (one(a_high, b_low) + both[rows:])


def call(kernel, shapes, *args, scalars=0):
    vmem = pl.BlockSpec(memory_space=pltpu.VMEM)
    smem = pl.BlockSpec(memory_space=pltpu.SMEM)
    single = not isinstance(shapes, (list, tuple))
    outs = [shapes] if single else list(shapes)
    got = pl.pallas_call(
        kernel,
        out_shape=[jax.ShapeDtypeStruct(s, F32) for s in map(tuple, (o.shape for o in outs))],
        in_specs=[smem] * scalars + [vmem] * (len(args) - scalars),
        out_specs=[vmem] * len(outs),
        compiler_params=pltpu.CompilerParams(vmem_limit_bytes=48 << 20),
    )(*args)
    return got[0] if single else got


def like(*shape):
    return jax.ShapeDtypeStruct(shape, F32)


def spread(index_ref, thin_ref, out_ref, *, width, ratio):
    row = lax.axis_index("row")
    ways_row = out_ref.shape[0]
    ways_col = ratio * ways_row
    share = out_ref.shape[2] // ratio
    blocks = share // width
    for p in range(ratio):
        column = row + p * ways_row
        offset = lax.rem(column + 2048 * ways_col - index_ref[0] - 1, ways_col) // ways_row
        for j in range(CORES * blocks):
            at = ratio * j * width
            piece = thin_ref[:, at : at + width]
            for i in range(1, ratio):
                piece = jnp.where(offset == i, thin_ref[:, at + i * width : at + (i + 1) * width], piece)
            to = p * share + j % blocks * width
            for i, r in enumerate(order(ways_row)):
                if r % CORES == j // blocks:
                    out_ref[i, :, to : to + width] = piece


def route(every_ref, thin_ref, out_ref):
    ways_row = every_ref.shape[0]
    ways_col = out_ref.shape[0]
    part = thin_ref.shape[1] // BLOCK
    share = out_ref.shape[2] - part
    for i, c in enumerate(order(ways_col)):
        p = c // ways_row
        source = order(ways_row).index(c % ways_row)
        x = place(c)
        out_ref[i, :, :share] = every_ref[source, :, p * share : (p + 1) * share]
        out_ref[i, :, share:] = thin_ref[:, x * part : (x + 1) * part]


def multiply(pair_ref, got_ref, trail_ref, adjoint_ref, out_ref, panel_ref, work_ref):
    ways_col, thin_cols, _ = got_ref.shape
    rows_here, cols = trail_ref.shape
    share = cols // CORES
    for i, c in enumerate(order(ways_col)):
        at = slice(c * thin_cols, (c + 1) * thin_cols)
        for core in range(CORES):
            work_ref[at, core * share : (core + 1) * share] = pair_ref[core, i, :, :share]
        panel_ref[at, :] = got_ref[i, :, share:]
    scaled = work_ref[...] * -2.0
    per_eight = 8 // thin_cols
    col = lax.axis_index("col")
    eight = pl.ds(pl.multiple_of(col // per_eight * 8, 8), 8)
    owner = lax.broadcasted_iota(jnp.int32, (8, rows_here // BLOCK), 0) // thin_cols
    part = rows_here // BLOCK
    product = dot(scaled, trail_ref[...], ((1,), (1,)))
    for x in range(BLOCK):
        at = slice(x * part, (x + 1) * part)
        out_ref[x] = product[:, at]
        added = jnp.concatenate([adjoint_ref[:, at]] * per_eight, axis=0)
        added = jnp.where(owner == lax.rem(col, per_eight), added, jnp.zeros_like(added))
        out_ref[x, eight, :] = out_ref[x, eight, :] + added


def gram(parts_ref, panel_ref, inv_ref, out_ref):
    ways_col, thin_cols, _ = out_ref.shape
    total = parts_ref[0]
    for x in range(1, BLOCK):
        total = total + parts_ref[x]
    total = dot(inv_ref[...].T, total, ((1,), (0,)))
    part = total.shape[1]
    diag = dot(-panel_ref[...], total, ((1,), (1,)))
    for i, c in enumerate(order(ways_col)):
        at = slice(c * thin_cols, (c + 1) * thin_cols)
        out_ref[i, :, :part] = total[at, :]
        out_ref[i, :, part:] = diag[at, :]


def finish(parts_ref, grad_ref, out_ref):
    ways_col = parts_ref.shape[0]
    part = grad_ref.shape[1] // BLOCK
    diag = None
    for i in range(BLOCK):
        total = None
        for j, c in enumerate(order(ways_col)):
            if place(c) == i:
                total = parts_ref[j] if total is None else total + parts_ref[j]
        grad_ref[:, i * part : (i + 1) * part] = total[:, :part]
        diag = total[:, part:] if diag is None else diag + total[:, part:]
    for r in range(out_ref.shape[0]):
        out_ref[r] = diag


def last(parts_ref, grad_ref, out_ref, grad_out_ref):
    grad_out_ref[...] = grad_ref[...]
    total = parts_ref[0]
    for r in range(1, parts_ref.shape[0]):
        total = total + parts_ref[r]
    out_ref[...] = total


def body(trail_adjoint, panel, panel_adjoint, inv_diag, panel_index):
    rows_here, thin_cols = panel.shape
    width = inv_diag.shape[0]
    ways_row = lax.axis_size("row")
    ways_col = lax.axis_size("col")
    cols = trail_adjoint.shape[1]
    part = rows_here // BLOCK
    rows, columns = [order(ways_row)], [order(ways_col)]
    groups = {}
    for c in range(ways_col):
        block = (c // Y_WAYS // BLOCK_X, c % Y_WAYS // BLOCK_Y)
        groups.setdefault(block, []).append(c)
    groups = [sorted(g, key=place) for g in groups.values()]
    thin = panel.T

    def spreading(*refs):
        spread(*refs, width=width, ratio=ways_col // ways_row)

    share = cols // CORES
    copies = call(spreading, like(ways_row, thin_cols, rows_here // CORES), panel_index, thin, scalars=1)
    sent = call(route, like(ways_col, thin_cols, share + part), exchange(copies, "row", rows), thin)
    got = exchange(sent, "col", columns)
    chips = [list(range(r, r + CORES)) for r in range(0, ways_row, CORES)]
    pair = lax.all_gather(jnp.concatenate([got, got[:, :, :128]], axis=2), "row", axis=0, axis_index_groups=chips)
    vmem = pl.BlockSpec(memory_space=pltpu.VMEM)
    parts, panel_rows = pl.pallas_call(
        multiply,
        out_shape=[like(BLOCK, width, part), like(width, part)],
        in_specs=[vmem] * 4,
        out_specs=[vmem] * 2,
        scratch_shapes=[pltpu.VMEM((width, cols), F32)],
        compiler_params=pltpu.CompilerParams(vmem_limit_bytes=48 << 20),
    )(pair, got, trail_adjoint, panel_adjoint.T)
    both = call(gram, like(ways_col, thin_cols, part + width), exchange(parts, "col", groups), panel_rows, inv_diag)
    grad, mine = call(
        finish, [like(thin_cols, rows_here), like(ways_row, thin_cols, width)], exchange(both, "col", columns)
    )
    diag, grad = call(last, [like(thin_cols, width), like(thin_cols, rows_here)], exchange(mine, "row", rows), grad)
    return (grad.T, diag.T)


def solution(mesh):
    in_specs = (P("row", "col"), P("row", "col"), P("row", "col"), P(), P())
    out_specs = (P("row", "col"), P(None, "col"))
    return jax.shard_map(body, mesh=mesh, in_specs=in_specs, out_specs=out_specs, check_vma=False)
```

```python
import jax
import jax.numpy as jnp
from jax import lax
from jax.experimental import pallas as pl
from jax.experimental.pallas import tpu as pltpu
from jax.sharding import PartitionSpec as P

Y_WAYS = 8
BLOCK_X, BLOCK_Y = 4, 2
BLOCK = BLOCK_X * BLOCK_Y
CORES = 2
F32 = jnp.float32


def order(ways):
    stride = 5 if ways > 16 else 3
    return [stride * i % ways for i in range(ways)]


def place(col):
    x, y = col // Y_WAYS, col % Y_WAYS
    return (x + y) % BLOCK_Y * BLOCK_X + x % BLOCK_X


def exchange(value, axis, groups=None):
    return lax.all_to_all(value, axis, split_axis=0, concat_axis=0, axis_index_groups=groups)


def halves(value):
    high = value.astype(jnp.bfloat16)
    low = (value - high.astype(F32)).astype(jnp.bfloat16)
    return high, low


def dot(a, b, contract):
    a_high, a_low = halves(a)
    b_high, b_low = halves(b)

    def one(p, q):
        return lax.dot_general(p, q, (contract, ((), ())), preferred_element_type=F32)

    rows = a.shape[0]
    both = one(jnp.concatenate([a_high, a_low], axis=0), b_high)
    return both[:rows] + (one(a_high, b_low) + both[rows:])


def call(kernel, shapes, *args, scalars=0):
    vmem = pl.BlockSpec(memory_space=pltpu.VMEM)
    smem = pl.BlockSpec(memory_space=pltpu.SMEM)
    single = not isinstance(shapes, (list, tuple))
    outs = [shapes] if single else list(shapes)
    got = pl.pallas_call(
        kernel,
        out_shape=[jax.ShapeDtypeStruct(s, F32) for s in map(tuple, (o.shape for o in outs))],
        in_specs=[smem] * scalars + [vmem] * (len(args) - scalars),
        out_specs=[vmem] * len(outs),
        compiler_params=pltpu.CompilerParams(vmem_limit_bytes=48 << 20),
    )(*args)
    return got[0] if single else got


def like(*shape):
    return jax.ShapeDtypeStruct(shape, F32)


def spread(index_ref, thin_ref, out_ref, *, width, ratio):
    row = lax.axis_index("row")
    ways_row = out_ref.shape[0]
    ways_col = ratio * ways_row
    share = out_ref.shape[2] // ratio
    blocks = share // width
    for p in range(ratio):
        column = row + p * ways_row
        offset = lax.rem(column + 2048 * ways_col - index_ref[0] - 1, ways_col) // ways_row
        for j in range(CORES * blocks):
            at = ratio * j * width
            piece = thin_ref[:, at : at + width]
            for i in range(1, ratio):
                piece = jnp.where(offset == i, thin_ref[:, at + i * width : at + (i + 1) * width], piece)
            to = p * share + j % blocks * width
            for i, r in enumerate(order(ways_row)):
                if r % CORES == j // blocks:
                    out_ref[i, :, to : to + width] = piece


def route(every_ref, thin_ref, out_ref):
    ways_row = every_ref.shape[0]
    ways_col = out_ref.shape[0]
    part = thin_ref.shape[1] // BLOCK
    share = out_ref.shape[2] - part
    for i, c in enumerate(order(ways_col)):
        p = c // ways_row
        source = order(ways_row).index(c % ways_row)
        x = place(c)
        out_ref[i, :, :share] = every_ref[source, :, p * share : (p + 1) * share]
        out_ref[i, :, share:] = thin_ref[:, x * part : (x + 1) * part]


def multiply(pair_ref, got_ref, trail_ref, adjoint_ref, out_ref, panel_ref, work_ref):
    ways_col, thin_cols, _ = got_ref.shape
    rows_here, cols = trail_ref.shape
    share = cols // CORES
    for i, c in enumerate(order(ways_col)):
        at = slice(c * thin_cols, (c + 1) * thin_cols)
        for core in range(CORES):
            work_ref[at, core * share : (core + 1) * share] = pair_ref[core, i, :, :share]
        panel_ref[at, :] = got_ref[i, :, share:]
    scaled = work_ref[...] * -2.0
    per_eight = 8 // thin_cols
    col = lax.axis_index("col")
    eight = pl.ds(pl.multiple_of(col // per_eight * 8, 8), 8)
    owner = lax.broadcasted_iota(jnp.int32, (8, rows_here // BLOCK), 0) // thin_cols
    part = rows_here // BLOCK
    product = dot(scaled, trail_ref[...], ((1,), (1,)))
    for x in range(BLOCK):
        at = slice(x * part, (x + 1) * part)
        out_ref[x] = product[:, at]
        added = jnp.concatenate([adjoint_ref[:, at]] * per_eight, axis=0)
        added = jnp.where(owner == lax.rem(col, per_eight), added, jnp.zeros_like(added))
        out_ref[x, eight, :] = out_ref[x, eight, :] + added


def gram(parts_ref, panel_ref, inv_ref, out_ref):
    ways_col, thin_cols, _ = out_ref.shape
    total = parts_ref[0]
    for x in range(1, BLOCK):
        total = total + parts_ref[x]
    total = dot(inv_ref[...].T, total, ((1,), (0,)))
    part = total.shape[1]
    diag = dot(-panel_ref[...], total, ((1,), (1,)))
    for i, c in enumerate(order(ways_col)):
        at = slice(c * thin_cols, (c + 1) * thin_cols)
        out_ref[i, :, :part] = total[at, :]
        out_ref[i, :, part:] = diag[at, :]


def finish(parts_ref, grad_ref, out_ref):
    ways_col = parts_ref.shape[0]
    part = grad_ref.shape[1] // BLOCK
    diag = None
    for i in range(BLOCK):
        total = None
        for j, c in enumerate(order(ways_col)):
            if place(c) == i:
                total = parts_ref[j] if total is None else total + parts_ref[j]
        grad_ref[:, i * part : (i + 1) * part] = total[:, :part]
        diag = total[:, part:] if diag is None else diag + total[:, part:]
    for r in range(out_ref.shape[0]):
        out_ref[r] = diag


def last(parts_ref, grad_ref, out_ref, grad_out_ref):
    grad_out_ref[...] = grad_ref[...]
    total = parts_ref[0]
    for r in range(1, parts_ref.shape[0]):
        total = total + parts_ref[r]
    out_ref[...] = total


def body(trail_adjoint, panel, panel_adjoint, inv_diag, panel_index):
    rows_here, thin_cols = panel.shape
    width = inv_diag.shape[0]
    ways_row = lax.axis_size("row")
    ways_col = lax.axis_size("col")
    cols = trail_adjoint.shape[1]
    part = rows_here // BLOCK
    rows, columns = [order(ways_row)], [order(ways_col)]
    groups = {}
    for c in range(ways_col):
        block = (c // Y_WAYS // BLOCK_X, c % Y_WAYS // BLOCK_Y)
        groups.setdefault(block, []).append(c)
    groups = [sorted(g, key=place) for g in groups.values()]
    thin = panel.T

    def spreading(*refs):
        spread(*refs, width=width, ratio=ways_col // ways_row)

    share = cols // CORES
    copies = call(spreading, like(ways_row, thin_cols, rows_here // CORES), panel_index, thin, scalars=1)
    sent = call(route, like(ways_col, thin_cols, share + part), exchange(copies, "row", rows), thin)
    got = exchange(sent, "col", columns)
    chips = [list(range(r, r + CORES)) for r in range(0, ways_row, CORES)]
    pair = lax.all_gather(jnp.concatenate([got, got[:, :, :128]], axis=2), "row", axis=0, axis_index_groups=chips)
    vmem = pl.BlockSpec(memory_space=pltpu.VMEM)
    parts, panel_rows = pl.pallas_call(
        multiply,
        out_shape=[like(BLOCK, width, part), like(width, part)],
        in_specs=[vmem] * 4,
        out_specs=[vmem] * 2,
        scratch_shapes=[pltpu.VMEM((width, cols), F32)],
        compiler_params=pltpu.CompilerParams(vmem_limit_bytes=48 << 20),
    )(pair, got, trail_adjoint, panel_adjoint.T)
    both = call(gram, like(ways_col, thin_cols, part + width), exchange(parts, "col", groups), panel_rows, inv_diag)
    grad, mine = call(
        finish, [like(thin_cols, rows_here), like(ways_row, thin_cols, width)], exchange(both, "col", columns)
    )
    diag, grad = call(last, [like(thin_cols, width), like(thin_cols, rows_here)], exchange(mine, "row", rows), grad)
    return (grad.T, diag.T)


def solution(mesh):
    in_specs = (P("row", "col"), P("row", "col"), P("row", "col"), P(), P())
    out_specs = (P("row", "col"), P(None, "col"))
    return jax.shard_map(body, mesh=mesh, in_specs=in_specs, out_specs=out_specs, check_vma=False)
```
